32 devices in a mesh: dp: 4 (over y, core), owner: 8 (over z, x).
Axes of the slice: x: 2, y: 2, z: 4, core: 2. Of those that a mesh axis runs over, the one named last changes fastest.
Arguments:
- activations: bfloat16 [8192, 8192], P('dp', 'owner'), may hold values from -6 to 6
- ffn_grads: bfloat16 [8192, 16384], P('dp', 'owner'), may hold values from -6 to 6
- lengths: int32 [4, 16], P('dp'), may hold values from 1 to 512, 2048 in all within a row
- sample_pos: int32 [4, 16, 16], P('dp'), may hold values from 0 to 1048575
Outputs:
- chol_in: float32 [8192, 1536], P('owner')
- chol_out: float32 [16384, 1536], P('owner')
The draws below stay inside these ranges and needn't reach their ends.
Inputs may be any that keep to these rules, and one draw needn't show every extreme that they name: Each dp index's document lengths sum to 2048; the longest is exactly 512.
All inputs are finite; a program needn't handle non-finite values.
Results may differ from the reference program's by a relative error of at most 0.0019.
Values may be sent and summed in bfloat16 or wider, within the bound.
No kernel may reach another device: no remote copies, remote signals or barrier semaphores. Data moves between devices by JAX's collectives and lax.ppermute only.
A program may use at most 192 MiB of HBM per device.

```python
import math
import jax
import jax.numpy as jnp
import numpy as np
from jax import lax

DIN = 8192
FFW = 16384
PB = 512
NPAN = 3
TOK_DP = 2048
DOCS = 16
SAMP_DOC = 16
K = 1536
TOKENS = 8192
N_DP = 4


def set_ends(entries, own_key, smallest, top_value):
    longest = entries.shape.index(max(entries.shape))
    spots = []
    for shift in (0, 1):
        where = [jax.random.randint(jax.random.fold_in(own_key, axis), (), 0, length) for axis, length in enumerate(entries.shape)]
        where[longest] = (where[longest] + shift) % entries.shape[longest]
        spots.append(tuple(where))
    return entries.at[spots[0]].set(smallest).at[spots[1]].set(top_value)


def shard_levels(own_key, dims, cuts, smallest, largest):
    level = 1.0
    for axis_at, shards_of in cuts:
        heights = jax.random.uniform(jax.random.fold_in(jax.random.fold_in(own_key, 6), axis_at), (shards_of,), jnp.float32, smallest / len(cuts), largest / len(cuts))
        level = level * jnp.repeat(jnp.exp(heights), dims[axis_at] // shards_of).reshape((-1,) + (1,) * (len(dims) - 1 - axis_at))
    return level


def split_up(amount, total, bound, lean):
    loads = [(1 << 20) // math.isqrt(rank ** lean) + 1 for rank in range(2, amount + 1)]
    spare, given = total - bound - (amount - 1), [1] * (amount - 1)
    while spare > 0:
        free = [i for i in range(amount - 1) if given[i] < bound]
        mass, remaining = sum([loads[i] for i in free]), spare
        for i in free:
            extra = min(bound - given[i], max(1, remaining * loads[i] // mass), spare)
            given[i] = given[i] + extra
            spare = spare - extra
    return np.array([bound] + given)


def uneven(rng, number_of, total, reach, slope):
    if number_of == 2:
        one = jax.random.randint(rng, (), max(1, total - reach), min(reach, total - 1) + 1)
        return jnp.stack([one, total - one])
    sizes = jnp.asarray(split_up(number_of, total, reach, slope), jnp.int32)
    couples = (number_of - 1) // 2
    giver, sink = sizes[1:1 + 2 * couples:2], sizes[2:2 + 2 * couples:2]
    room = jnp.minimum(giver - 1, reach - sink)
    moved = jax.random.randint(jax.random.fold_in(rng, 1), (couples,), 0, 1 << 20) % (room + 1)
    sizes = sizes.at[1:1 + 2 * couples:2].set(giver - moved).at[2:2 + 2 * couples:2].set(sink + moved)
    return sizes[jax.random.permutation(jax.random.fold_in(rng, 2), number_of)]


def noise(key, dims, deviation, reach, shards=(), kind=jnp.bfloat16):
    gain = shard_levels(key, dims, shards, -0.22, 0.18) if shards else 1.0
    values = jax.random.normal(key, dims, jnp.float32) * deviation * gain
    return jnp.minimum(jnp.maximum(values, -reach), reach).astype(kind)


def setup_inputs(seed: int = 0) -> dict:
    splits = jax.random.split(jax.random.key(seed), 5)
    activations = noise(splits[0], (TOKENS, DIN), 1.0, 6.0, ((0, 4), (1, 8)))
    ffn_grads = noise(splits[1], (TOKENS, FFW), 1.0, 6.0, ((0, 4), (1, 8)))
    lengths = jax.vmap(lambda own: uneven(own, DOCS, TOK_DP, TOK_DP // 4, 2))(jax.random.split(splits[2], N_DP)).reshape((N_DP, DOCS)).astype(jnp.int32)
    sample_pos = set_ends(jax.random.randint(splits[3], (N_DP, DOCS, SAMP_DOC), 0, 1048576), jax.random.fold_in(splits[3], 1), 0, 1048575).astype(jnp.int32)
    return dict(activations=activations, ffn_grads=ffn_grads, lengths=lengths, sample_pos=sample_pos)


DAMPING = 0.1

def gram_of(values, row_index, weight, width):
    sampled = jnp.take(values, row_index, axis=0)
    scaled = (weight[:, None] * sampled.astype(jnp.float32)).astype(jnp.bfloat16)
    gram = jnp.dot(scaled.T.astype(jnp.float32), sampled[:, :K].astype(jnp.float32), preferred_element_type=jnp.float32)
    return gram + DAMPING * jnp.eye(width, K, dtype=jnp.float32)

def factorize(gram):
    height = gram.shape[0]
    triangle = jnp.zeros_like(gram)
    global_row = jnp.arange(height, dtype=jnp.int32)
    for column in range(NPAN):
        first_col = column * PB
        end_col = first_col + PB
        previous = triangle[first_col:end_col, :first_col]
        pivot_in = gram[first_col:end_col, first_col:end_col] - jnp.dot(previous, previous.T, precision=lax.Precision.HIGHEST)
        pivot = jnp.linalg.cholesky(pivot_in)
        residual = gram[:, first_col:end_col] - jnp.dot(triangle[:, :first_col], previous.T, precision=lax.Precision.HIGHEST)
        solved = lax.linalg.triangular_solve(pivot, residual, left_side=False, lower=True, transpose_a=True)
        inside = jnp.take(pivot, jnp.clip(global_row - first_col, 0, PB - 1), axis=0)
        solved = jnp.where((global_row < first_col)[:, None], 0.0, jnp.where((global_row < end_col)[:, None], inside, solved))
        triangle = triangle.at[:, first_col:end_col].set(solved)
    return triangle

def reference(activations, ffn_grads, lengths, sample_pos):
    doc_start = jnp.cumsum(lengths, axis=1) - lengths
    offsets = (jnp.arange(N_DP, dtype=jnp.int32) * TOK_DP)[:, None, None]
    row_index = (offsets + doc_start[:, :, None] + jnp.remainder(sample_pos, lengths[:, :, None])).reshape(-1).astype(jnp.int32)
    weight = jnp.broadcast_to((lengths.astype(jnp.float32) / (SAMP_DOC * TOKENS))[:, :, None], sample_pos.shape).reshape(-1)
    gram_in = gram_of(activations, row_index, weight, DIN)
    gram_out = gram_of(ffn_grads, row_index, weight, FFW)
    return (factorize(gram_in), factorize(gram_out))
```

```python
import functools

import jax
import jax.numpy as jnp
from jax import lax
from jax.experimental import pallas as pl
from jax.experimental.pallas import tpu as pltpu
from jax.sharding import PartitionSpec as P

PB = 512
NPAN = 3
SAMP_DOC = 16
DAMPING = 0.1
BLK = 128
TILE = 256
F32 = jnp.float32
BF16 = jnp.bfloat16
AXES = ("dp", "owner")


def split(x):
    hi = x.astype(BF16)
    return hi, (x - hi.astype(F32)).astype(BF16)


def mm(a, b, ca, cb):
    return lax.dot_general(a, b, (((ca,), (cb,)), ((), ())), preferred_element_type=F32)


def mm3(a, b, ca, cb):
    (ah, al), (bh, bl) = a, b
    return mm(ah, bh, ca, cb) + (mm(ah, bl, ca, cb) + mm(al, bh, ca, cb))


def recip(d):
    r = pltpu.reciprocal(d, approx=True)
    return r * (2.0 - d * r)


def factor_block(a):
    lane = lax.broadcasted_iota(jnp.int32, (8, BLK), 1)
    sub = lax.broadcasted_iota(jnp.int32, (8, BLK), 0)
    groups = BLK // 8
    rows_of = [a[8 * g : 8 * g + 8] for g in range(groups)]
    upper, inverse = [], []

    def fill(x):
        return jnp.broadcast_to(x, (8, BLK))

    for g in range(groups):
        top, c0 = rows_of[g], 8 * g
        rr = [fill(top[i : i + 1, :]) for i in range(8)]
        e = {(i, j): fill(rr[i][:, c0 + j : c0 + j + 1]) for i in range(8) for j in range(i + 1)}
        below = range(g + 1, groups)
        col = {(h, j): fill(rows_of[h][:, c0 + j : c0 + j + 1]) for h in below for j in range(8)}
        mult, src = {}, {}
        for k in range(0, 8, 2):
            p, q, r = e[k, k], e[k + 1, k], e[k + 1, k + 1]
            inv = recip(p * r - q * q)
            pi, qi, ri = p * inv, q * inv, r * inv
            at0, at1 = lane == c0 + k, lane == c0 + k + 1
            s0 = jnp.where(at0, 1.0, jnp.where(at1, 0.0, rr[k]))
            s1 = jnp.where(at1, 1.0, jnp.where(at0, 0.0, rr[k + 1]))
            for i in range(k + 2, 8):
                x, y = e[i, k], e[i, k + 1]
                m0, m1 = (x * r - y * q) * inv, (y * p - x * q) * inv
                for j in range(k + 2, i + 1):
                    e[i, j] = e[i, j] - (m0 * e[j, k] + m1 * e[j, k + 1])
                rr[i] = jnp.where(at0 | at1, 0.0, rr[i]) - (m0 * s0 + m1 * s1)
            later = (lane > c0 + k + 1) & (lane < c0 + 8)
            src[k], src[k + 1] = jnp.where(later, 0.0, s0), jnp.where(later, 0.0, s1)
            for h in below:
                x, y = col[h, k], col[h, k + 1]
                m0, m1 = x * ri - y * qi, y * pi - x * qi
                mult[h, k], mult[h, k + 1] = m0, m1
                for j in range(k + 2, 8):
                    col[h, j] = col[h, j] - (m0 * e[j, k] + m1 * e[j, k + 1])
        for h in below:
            acc = jnp.where((lane >= c0) & (lane < c0 + 8), 0.0, rows_of[h])
            for j in range(0, 8, 2):
                acc = acc - (mult[h, j] * src[j] + mult[h, j + 1] * src[j + 1])
            rows_of[h] = acc
        done = scale = None
        for k in range(8):
            if k % 2 == 0:
                d, row = e[k, k], rr[k]
            else:
                t = e[k, k - 1] / e[k - 1, k - 1]
                d = e[k, k] - t * e[k, k - 1]
                before = lane == c0 + k - 1
                row = jnp.where(before, 0.0, rr[k]) - t * jnp.where(before, 1.0, rr[k - 1])
            s = lax.rsqrt(d)
            row = row * s
            done = row if k == 0 else jnp.where(sub == k, row, done)
            scale = s if k == 0 else jnp.where(sub == k, s, scale)
        diag = c0 + sub
        upper.append(jnp.where(lane >= diag, done, 0.0))
        inverse.append(jnp.where(lane < diag, done, jnp.where(lane == diag, scale, 0.0)))
    return jnp.concatenate(upper, 0), jnp.concatenate(inverse, 0)


def panel_kernel(panel, *refs):
    w_ref, weight_ref = refs[:2]
    prev = refs[2 : 2 + 2 * panel]
    vh_ref, vl_ref, l_ref, sw, a, z, y, lq = refs[2 + 2 * panel :]
    samples = w_ref.shape[0]
    chunk = TILE

    @pl.loop(0, samples // chunk)
    def _(i):
        at = pl.ds(pl.multiple_of(i * chunk, chunk), chunk)
        w = w_ref[at, :].astype(F32)
        sw[at, :] = (weight_ref[at, :] * w).astype(BF16)
        y[at, :] = w

    row = lax.broadcasted_iota(jnp.int32, (PB, PB), 0)
    column = lax.broadcasted_iota(jnp.int32, (PB, PB), 1)
    eye = (row == column).astype(F32)
    gram = mm(sw[...], w_ref[...], 0, 0) + mm(w_ref[...], sw[...], 0, 0)
    a[...] = 0.5 * gram + DAMPING * eye
    z[...] = eye
    for q in range(panel):
        vh, vl = prev[2 * q], prev[2 * q + 1]
        lh, ll = split(mm(sw[...], vh[...], 0, 0) + mm(sw[...], vl[...], 0, 0))
        lq[0], lq[1] = lh, ll
        a[...] -= mm3((lh, ll), (lh, ll), 1, 1)

        @pl.loop(0, samples // chunk)
        def _(i):
            at = pl.ds(pl.multiple_of(i * chunk, chunk), chunk)
            y[at, :] -= mm3((vh[at, :], vl[at, :]), (lq[0], lq[1]), 1, 1)

    l_ref[...] = jnp.zeros((PB, PB), F32)

    @pl.loop(0, PB // BLK)
    def _(b):
        at = pl.ds(pl.multiple_of(b * BLK, BLK), BLK)
        upper, inverse = factor_block(a[at, at])
        x = split(inverse)
        below = lax.broadcasted_iota(jnp.int32, (PB, BLK), 0) >= (b + 1) * BLK
        lcol = jnp.where(below, mm3(split(a[:, at]), x, 1, 1), 0.0)
        l_ref[:, at] = lcol
        l_ref[at, at] = upper.T
        lcol = split(lcol)
        a[...] -= mm3(lcol, lcol, 1, 1)
        zb = mm3(x, split(z[at, :]), 1, 0)
        z[...] -= mm3(lcol, split(zb), 1, 0)
        z[at, :] = zb

    zz = split(z[...])
    lq[0], lq[1] = zz

    @pl.loop(0, samples // chunk)
    def _(i):
        at = pl.ds(pl.multiple_of(i * chunk, chunk), chunk)
        v = mm3(split(y[at, :]), (lq[0], lq[1]), 1, 1)
        vh_ref[at, :], vl_ref[at, :] = split(v)


def factor_panel(window, weight, done):
    panel, samples = len(done), window.shape[0]
    vshape = jax.ShapeDtypeStruct((samples, PB), BF16)
    return pl.pallas_call(
        functools.partial(panel_kernel, panel),
        out_shape=(vshape, vshape, jax.ShapeDtypeStruct((PB, PB), F32)),
        scratch_shapes=[
            pltpu.VMEM((samples, PB), BF16),
            pltpu.VMEM((PB, PB), F32),
            pltpu.VMEM((PB, PB), F32),
            pltpu.VMEM((samples, PB), F32),
            pltpu.VMEM((2, PB, PB), BF16),
        ],
        compiler_params=pltpu.CompilerParams(vmem_limit_bytes=48 << 20),
        name=f"factor_panel_{panel}",
    )(window, weight, *[part for v in done for part in v[:2]])


def rows_kernel(pos_ref, s_ref, *refs):
    parts, (out_ref, buf, lbuf, sem) = refs[:-4], refs[-4:]
    own, other = parts[:9], parts[9:]
    step = pl.program_id(0)

    def copies(group):
        made = []
        for p in range(NPAN):
            made.append((group[3 * p], buf.at[p, 0]))
            made.append((group[3 * p + 1], buf.at[p, 1]))
            made.append((group[3 * p + 2], lbuf.at[p]))
        return [pltpu.make_async_copy(s, d, sem.at[i]) for i, (s, d) in enumerate(made)]

    for mine, group in ((1, own), (0, other)):

        @pl.when((step == 0) & (pos_ref[1] == mine))
        def _():
            for copy in copies(group):
                copy.start()
            for copy in copies(group):
                copy.wait()

    first = pos_ref[0] + step * TILE
    for p in range(NPAN):
        cols = slice(p * PB, (p + 1) * PB)

        @pl.when(first >= (p + 1) * PB)
        def _():
            s = s_ref[...]
            out_ref[:, cols] = mm(s, buf[p, 0], 0, 0) + mm(s, buf[p, 1], 0, 0)

        @pl.when((first >= p * PB) & (first < (p + 1) * PB))
        def _():
            at = pl.multiple_of(jnp.clip(first - p * PB, 0, PB - TILE), TILE)
            out_ref[:, cols] = lbuf[p, pl.ds(at, TILE), :]

        @pl.when(first < p * PB)
        def _():
            out_ref[:, cols] = jnp.zeros((TILE, PB), F32)


def factor_rows(scaled, position, own, other):
    samples, height = scaled.shape
    parts = [x for group in (own, other) for v in group for x in v]
    anywhere = pl.BlockSpec(memory_space=pl.ANY)
    return pl.pallas_call(
        rows_kernel,
        grid_spec=pltpu.PrefetchScalarGridSpec(
            num_scalar_prefetch=1,
            grid=(height // TILE,),
            in_specs=[pl.BlockSpec((samples, TILE), lambda i, pos: (0, i))] + [anywhere] * len(parts),
            out_specs=pl.BlockSpec((TILE, NPAN * PB), lambda i, pos: (i, 0)),
            scratch_shapes=[
                pltpu.VMEM((NPAN, 2, samples, PB), BF16),
                pltpu.VMEM((NPAN, PB, PB), F32),
                pltpu.SemaphoreType.DMA((3 * NPAN,)),
            ],
        ),
        out_shape=jax.ShapeDtypeStruct((height, NPAN * PB), F32),
        compiler_params=pltpu.CompilerParams(vmem_limit_bytes=48 << 20),
        name="factor_rows",
    )(position, scaled, *parts)


class Grid:
    def __init__(self, n_dp, n_owner):
        self.ny, self.no = n_dp // 2, n_owner
        self.nz = 4 if n_owner % 4 == 0 else 1
        self.nx = n_owner // self.nz
        dp, owner = lax.axis_index("dp"), lax.axis_index("owner")
        self.y, self.core = dp // 2, dp % 2
        self.z, self.x = owner // self.nx, owner % self.nx

    def at(self, y, core, z, x):
        return (2 * y + core) * self.no + z * self.nx + x

    def everywhere(self):
        return [
            (y, c, z, x)
            for y in range(self.ny)
            for c in range(2)
            for z in range(self.nz)
            for x in range(self.nx)
        ]

    def send(self, value, moves):
        return lax.ppermute(value, AXES, [(self.at(*a), self.at(*b)) for a, b in moves])

    def other_core(self, value):
        return self.send(value, [((y, c, z, x), (y, 1 - c, z, x)) for y, c, z, x in self.everywhere()])

    def by_core(self, pair):
        return jnp.where(self.core == 0, pair[0], pair[1])

    def gather(self, value, size, index, move):
        parts = [value]
        for k in range(1, size):
            parts.append(self.send(value, move(k)))
        if size == 2:
            swapped = index == 1
            return jnp.concatenate(
                [jnp.where(swapped, parts[1], parts[0]), jnp.where(swapped, parts[0], parts[1])], 0
            )
        rows = value.shape[0]
        both = jnp.concatenate(parts + parts, 0)
        start = ((size - index) % size) * rows
        return lax.dynamic_slice_in_dim(both, start, size * rows, 0)

    def gather_x(self, value):
        return self.gather(
            value,
            self.nx,
            self.x,
            lambda k: [((y, c, z, (x + k) % self.nx), (y, c, z, x)) for y, c, z, x in self.everywhere()],
        )

    def gather_y(self, value):
        return self.gather(
            value,
            self.ny,
            self.y,
            lambda k: [(((y + k) % self.ny, c, z, x), (y, c, z, x)) for y, c, z, x in self.everywhere()],
        )


def spread_window(grid, pieces, roots):
    ny, nz, nx = grid.ny, grid.nz, grid.nx
    keep, give = grid.by_core(pieces), grid.by_core(pieces[::-1])
    got = grid.send(
        give,
        [((y, c, *divmod(roots[1 - c], nx)), (y, 1 - c, *divmod(roots[1 - c], nx))) for y in range(ny) for c in range(2)],
    )
    low = grid.core == 0
    whole = jnp.concatenate([jnp.where(low, keep, got), jnp.where(low, got, keep)], 0)
    rows = whole.shape[0] // nx
    zr = [r // nx for r in roots]
    xr = [r % nx for r in roots]
    root_x = jnp.where(low, xr[0], xr[1])
    root_z = jnp.where(low, zr[0], zr[1])
    part = lax.dynamic_slice_in_dim(whole, grid.x * rows, rows, 0)
    for k in range(1, nx):
        piece = lax.dynamic_slice_in_dim(whole, ((root_x + k) % nx) * rows, rows, 0)
        got = grid.send(
            piece,
            [((y, c, zr[c], xr[c]), (y, c, zr[c], (xr[c] + k) % nx)) for y in range(ny) for c in range(2)],
        )
        part = jnp.where((grid.x - root_x + nx) % nx == k, got, part)
    mine = part
    for k in range(1, nz):
        got = grid.send(
            mine,
            [
                ((y, c, zr[c], x), (y, c, (zr[c] + k) % nz, x))
                for y in range(ny)
                for c in range(2)
                for x in range(nx)
            ],
        )
        part = jnp.where((grid.z - root_z + nz) % nz == k, got, part)
    return grid.gather_y(grid.gather_x(part))


def local(activations, ffn_grads, lengths, sample_pos):
    n_dp, n_owner = lax.axis_size("dp"), lax.axis_size("owner")
    tokens = activations.shape[0]
    total = tokens * n_dp
    grid = Grid(n_dp, n_owner)
    doc_len = lengths[0]
    doc_start = jnp.cumsum(doc_len) - doc_len
    row_index = (doc_start[:, None] + jnp.remainder(sample_pos[0], doc_len[:, None])).reshape(-1)

    def weights(lens):
        scale = lens.astype(F32) / (SAMP_DOC * total)
        return jnp.broadcast_to(scale[..., None], (*lens.shape, SAMP_DOC)).reshape(-1, 1)

    weight = weights(doc_len)
    every_weight = weights(lax.all_gather(doc_len, "dp"))
    hot = (row_index[:, None] == jnp.arange(tokens, dtype=jnp.int32)[None, :]).astype(BF16)
    sampled = [jnp.dot(hot, v, preferred_element_type=F32).astype(BF16) for v in (activations, ffn_grads)]
    scaled = [(weight * s.astype(F32)).astype(BF16) for s in sampled]

    windows = []
    for panel in range(NPAN):
        first = panel * PB
        roots = [first // s.shape[1] for s in sampled]
        pieces = [s[:, first % s.shape[1] : first % s.shape[1] + PB] for s in sampled]
        windows.append(spread_window(grid, pieces, roots))

    own, other = [], []
    for panel in range(NPAN):
        done = factor_panel(windows[panel], every_weight, own)
        own.append(done)
        other.append([grid.other_core(x) for x in done])

    rows = jnp.concatenate(scaled, axis=1)
    rows = grid.gather_y(grid.gather(rows, 2, grid.core, lambda k: [((y, 1 - c, z, x), (y, c, z, x)) for y, c, z, x in grid.everywhere()]))
    width = scaled[0].shape[1]
    every = [rows[:, :width], rows[:, width:]]
    outs = []
    for m in range(2):
        height = every[m].shape[1]
        position = jnp.stack([lax.axis_index("owner") * height, (grid.core == m).astype(jnp.int32)])
        outs.append(factor_rows(every[m], position.astype(jnp.int32), own, other))
    return tuple(outs)


def solution(mesh):
    return jax.shard_map(
        local,
        mesh=mesh,
        in_specs=(P("dp", "owner"), P("dp", "owner"), P("dp", None), P("dp", None, None)),
        out_specs=(P("owner", None), P("owner", None)),
        check_vma=False,
    )
```

```python
import functools

import jax
import jax.numpy as jnp
from jax import lax
from jax.experimental import pallas as pl
from jax.experimental.pallas import tpu as pltpu
from jax.sharding import PartitionSpec as P

PB = 512
NPAN = 3
SAMP_DOC = 16
DAMPING = 0.1
BLK = 128
TILE = 256
F32 = jnp.float32
BF16 = jnp.bfloat16
AXES = ("dp", "owner")


def split(x):
    hi = x.astype(BF16)
    return hi, (x - hi.astype(F32)).astype(BF16)


def mm(a, b, ca, cb):
    return lax.dot_general(a, b, (((ca,), (cb,)), ((), ())), preferred_element_type=F32)


def mm3(a, b, ca, cb):
    (ah, al), (bh, bl) = a, b
    return mm(jnp.concatenate([ah, ah, al], ca), jnp.concatenate([bh, bl, bh], cb), ca, cb)


def recip(d):
    r = pltpu.reciprocal(d, approx=True)
    return r * (2.0 - d * r)


def factor_block(a):
    lane = lax.broadcasted_iota(jnp.int32, (8, BLK), 1)
    sub = lax.broadcasted_iota(jnp.int32, (8, BLK), 0)
    groups = BLK // 8
    rows_of = [a[8 * g : 8 * g + 8] for g in range(groups)]
    upper, inverse = [], []

    def fill(x):
        return jnp.broadcast_to(x, (8, BLK))

    for g in range(groups):
        top, c0 = rows_of[g], 8 * g
        rr = [fill(top[i : i + 1, :]) for i in range(8)]
        e = {(i, j): fill(rr[i][:, c0 + j : c0 + j + 1]) for i in range(8) for j in range(i + 1)}
        below = range(g + 1, groups)
        unit, mult, solved = {}, {}, {}
        for k in range(0, 8, 2):
            p, q, r = e[k, k], e[k + 1, k], e[k + 1, k + 1]
            inv = recip(p * r - q * q)
            at0, at1 = lane == c0 + k, lane == c0 + k + 1
            s0 = jnp.where(at0, 1.0, jnp.where(at1, 0.0, rr[k]))
            s1 = jnp.where(at1, 1.0, jnp.where(at0, 0.0, rr[k + 1]))
            for i in range(k + 2, 8):
                x, y = e[i, k], e[i, k + 1]
                m0, m1 = (x * r - y * q) * inv, (y * p - x * q) * inv
                mult[i, k], mult[i, k + 1] = m0, m1
                for j in range(k + 2, i + 1):
                    e[i, j] = e[i, j] - (m0 * e[j, k] + m1 * e[j, k + 1])
                rr[i] = jnp.where(at0 | at1, 0.0, rr[i]) - (m0 * s0 + m1 * s1)
            later = (lane > c0 + k + 1) & (lane < c0 + 8)
            s0, s1 = jnp.where(later, 0.0, s0), jnp.where(later, 0.0, s1)
            unit[k], unit[k + 1] = (s0 * r - s1 * q) * inv, (s1 * p - s0 * q) * inv
        if g + 1 < groups:
            for k in range(6, -1, -2):
                for c in (k, k + 1):
                    t = unit[c]
                    for i in range(6, k, -2):
                        t = t - (mult[i, c] * solved[i] + mult[i + 1, c] * solved[i + 1])
                    solved[c] = t
        for h in below:
            col = [fill(rows_of[h][:, c0 + j : c0 + j + 1]) for j in range(8)]
            base = jnp.where((lane >= c0) & (lane < c0 + 8), 0.0, rows_of[h])
            pair = [col[j] * solved[j] + col[j + 1] * solved[j + 1] for j in range(0, 8, 2)]
            rows_of[h] = base - ((pair[0] + pair[1]) + (pair[2] + pair[3]))
        done = scale = None
        for k in range(8):
            if k % 2 == 0:
                d, row = e[k, k], rr[k]
            else:
                t = e[k, k - 1] / e[k - 1, k - 1]
                d = e[k, k] - t * e[k, k - 1]
                before = lane == c0 + k - 1
                row = jnp.where(before, 0.0, rr[k]) - t * jnp.where(before, 1.0, rr[k - 1])
            s = lax.rsqrt(d)
            row = row * s
            done = row if k == 0 else jnp.where(sub == k, row, done)
            scale = s if k == 0 else jnp.where(sub == k, s, scale)
        diag = c0 + sub
        upper.append(jnp.where(lane >= diag, done, 0.0))
        inverse.append(jnp.where(lane < diag, done, jnp.where(lane == diag, scale, 0.0)))
    return jnp.concatenate(upper, 0), jnp.concatenate(inverse, 0)


def panel_kernel(panel, blocks, place_ref, *refs):
    w_refs, weight_ref = refs[:blocks], refs[blocks]
    prev = refs[blocks + 1 : blocks + 1 + panel]
    v_ref, l_ref, w, swt, a, y, lq, xs = refs[blocks + 1 + panel :]
    samples = w.shape[0]
    known_rows = slice(0, samples)
    rows = samples // blocks
    half, apart = rows // 2, place_ref[blocks]
    for i in range(blocks):
        for core in range(2):
            at = pl.ds(pl.multiple_of(place_ref[i] + core * apart, half), half)
            w[at, :] = w_refs[i][core * half : (core + 1) * half, :]

    for i in range(samples // TILE):
        at = slice(i * TILE, (i + 1) * TILE)
        swt[:, at] = (weight_ref[at, :] * w[at, :].astype(F32)).astype(BF16).T

    gram = mm(swt[...], w[...], 1, 0)
    row = lax.broadcasted_iota(jnp.int32, (PB, PB), 0)
    column = lax.broadcasted_iota(jnp.int32, (PB, PB), 1)
    a[...] = 0.5 * (gram + gram.T) + jnp.where(row == column, DAMPING, 0.0)
    for q in range(panel):
        lpq = mm(swt[...], prev[q][0, known_rows], 1, 0) + mm(swt[...], prev[q][1, known_rows], 1, 0)
        lq[q, 0], lq[q, 1] = split(lpq)
    for j in range(PB // BLK):
        at, below = slice(j * BLK, (j + 1) * BLK), slice(j * BLK, PB)
        for q in range(panel):
            a[below, at] -= mm3((lq[q, 0, below], lq[q, 1, below]), (lq[q, 0, at], lq[q, 1, at]), 1, 1)

    l_ref[...] = jnp.zeros((PB, PB), F32)
    v_ref[...] = jnp.zeros(v_ref.shape, BF16)
    xs[...] = jnp.zeros(xs.shape, BF16)
    y[...] = jnp.zeros(y.shape, F32)

    def finish(at):
        found = y[...] - mm3((v_ref[0, known_rows], v_ref[1, known_rows]), split(l_ref[at, :]), 1, 1)
        v_ref[0, known_rows, at], v_ref[1, known_rows, at] = split(mm3(split(found), (xs[0], xs[1]), 1, 1))

    @pl.loop(0, PB // BLK)
    def _(b):
        at = pl.ds(pl.multiple_of(b * BLK, BLK), BLK)
        finish(pl.ds(pl.multiple_of(jnp.maximum(b - 1, 0) * BLK, BLK), BLK))
        own = w[:, at].astype(F32)
        for q in range(panel):
            own -= mm3((prev[q][0, known_rows], prev[q][1, known_rows]), (lq[q, 0, at, :], lq[q, 1, at, :]), 1, 1)
        y[...] = own
        upper, inverse = factor_block(a[at, at])
        x = split(inverse)
        xs[0], xs[1] = x
        l_ref[at, at] = upper.T
        for known in range(PB // BLK - 1):

            @pl.when(b == known)
            def _():
                done, below = slice(known * BLK, (known + 1) * BLK), slice((known + 1) * BLK, PB)
                lcol = mm3(split(a[below, done]), x, 1, 1)
                l_ref[below, done] = lcol
                lh, ll = split(lcol)
                for j in range(PB // BLK - known - 1):
                    c, r = slice(j * BLK, (j + 1) * BLK), slice((known + 1 + j) * BLK, PB)
                    to = slice((known + 1 + j) * BLK, (known + 2 + j) * BLK)
                    a[r, to] -= mm3((lh[j * BLK :], ll[j * BLK :]), (lh[c], ll[c]), 1, 1)

    finish(slice(PB - BLK, PB))
    v_ref[0, samples:, :], v_ref[1, samples:, :] = split(l_ref[...])


def factor_panel(window, column, places, weight, done):
    panel, samples = len(done), weight.shape[0]
    vshape = jax.ShapeDtypeStruct((2, samples + PB, PB), BF16)

    def whole(x):
        return pl.BlockSpec(x.shape, lambda i, place: (0,) * len(x.shape))

    return pl.pallas_call(
        functools.partial(panel_kernel, panel, len(window)),
        grid_spec=pltpu.PrefetchScalarGridSpec(
            num_scalar_prefetch=1,
            grid=(1,),
            in_specs=[pl.BlockSpec((b.shape[0], PB), lambda i, place: (0, column)) for b in window]
            + [whole(x) for x in (weight, *done)],
            out_specs=whole(vshape),
            scratch_shapes=[
                pltpu.VMEM((PB, PB), F32),
                pltpu.VMEM((samples, PB), BF16),
                pltpu.VMEM((PB, samples), BF16),
                pltpu.VMEM((PB, PB), F32),
                pltpu.VMEM((samples, BLK), F32),
                pltpu.VMEM((max(panel, 1), 2, PB, PB), BF16),
                pltpu.VMEM((2, BLK, BLK), BF16),
            ],
        ),
        out_shape=vshape,
        compiler_params=pltpu.CompilerParams(vmem_limit_bytes=(12 << 20) + (20 << 10) * samples),
        cost_estimate=pl.CostEstimate(flops=int(3e10), transcendentals=0, bytes_accessed=int(1e7)),
        name=f"factor_panel_{panel}",
    )(places, *window, weight, *done)


def rows_kernel(blocks, panels, tiles, pos_ref, *refs):
    n = len(panels)
    s_refs, own, other = refs[:blocks], refs[blocks : blocks + n], refs[blocks + n : blocks + 2 * n]
    out_refs, (buf, sem) = refs[-4:-2], refs[-2:]
    step = pl.program_id(0)
    rows = s_refs[0].shape[0]
    samples = rows * blocks

    def copies(m, group):
        return [pltpu.make_async_copy(group[p], buf.at[m, p], sem.at[m, p]) for p in range(n)]

    @pl.when(step == 0)
    def _():
        for core in range(2):

            @pl.when(pos_ref[0] == core)
            def _():
                for m in range(2):
                    for copy in copies(m, own if m == core else other):
                        copy.start()

    for m in range(2):

        @pl.when(step == (0 if m == 0 else tiles[0]))
        def _():
            for copy in copies(m, own):
                copy.wait()

        @pl.when((step < tiles[0]) if m == 0 else (step >= tiles[0]))
        def _():
            out_ref = out_refs[m]
            first = pos_ref[1 + m] + (step if m == 0 else step - tiles[0]) * TILE
            for i, p in enumerate(panels):
                cols = slice(i * PB, (i + 1) * PB)

                @pl.when(first >= (p + 1) * PB)
                def _():
                    total = None
                    for j in range(blocks):
                        s = s_refs[j][...]
                        at = pl.ds(pl.multiple_of(pos_ref[3 + j], rows), rows)
                        term = mm(s, buf[m, i, 0, at, :], 0, 0) + mm(s, buf[m, i, 1, at, :], 0, 0)
                        total = term if total is None else total + term
                    out_ref[:, cols] = total

                @pl.when((first >= p * PB) & (first < (p + 1) * PB))
                def _():
                    at = pl.multiple_of(samples + jnp.clip(first - p * PB, 0, PB - TILE), TILE)
                    at = pl.ds(at, TILE)
                    out_ref[:, cols] = buf[m, i, 0, at, :].astype(F32) + buf[m, i, 1, at, :].astype(F32)

                @pl.when(first < p * PB)
                def _():
                    out_ref[:, cols] = jnp.zeros((TILE, PB), F32)


def factor_rows(scaled, heights, panels, position, own, other, into):
    n = len(panels)
    parts = [group[p] for group in (own, other) for p in panels]
    anywhere = pl.BlockSpec(memory_space=pl.ANY)
    tiles = [h // TILE for h in heights]
    column = panels[0] // n

    def out_tile(m):
        if m == 0:
            return lambda i, pos: (jnp.minimum(i, tiles[0] - 1), column)
        return lambda i, pos: (jnp.maximum(i - tiles[0], 0), column)

    out_shape = [jax.ShapeDtypeStruct((h, NPAN * PB), F32) for h in heights]
    first_into = 1 + len(scaled) + len(parts)
    return pl.pallas_call(
        functools.partial(rows_kernel, len(scaled), panels, tiles),
        grid_spec=pltpu.PrefetchScalarGridSpec(
            num_scalar_prefetch=1,
            grid=(sum(tiles),),
            in_specs=[pl.BlockSpec((s.shape[0], TILE), lambda i, pos: (0, i)) for s in scaled]
            + [anywhere] * (len(parts) + len(into)),
            out_specs=[pl.BlockSpec((TILE, n * PB), out_tile(m)) for m in range(2)],
            scratch_shapes=[
                pltpu.VMEM((2, n, *own[0].shape), BF16),
                pltpu.SemaphoreType.DMA((2, n)),
            ],
        ),
        out_shape=out_shape,
        input_output_aliases={first_into + m: m for m in range(len(into))},
        compiler_params=pltpu.CompilerParams(vmem_limit_bytes=(20 << 20) + (16 << 10) * own[0].shape[1]),
        name=f"factor_rows_{panels[0]}",
    )(position, *scaled, *parts, *into)


class Grid:
    def __init__(self, n_dp, n_owner):
        self.ny, self.no = n_dp // 2, n_owner
        self.nz = 4 if n_owner % 4 == 0 else 1
        self.nx = n_owner // self.nz
        dp, owner = lax.axis_index("dp"), lax.axis_index("owner")
        self.y, self.core = dp // 2, dp % 2
        self.z, self.x = owner // self.nx, owner % self.nx

    def send(self, value, move):
        moves = []
        for y in range(self.ny):
            for c in range(2):
                for z in range(self.nz):
                    for x in range(self.nx):
                        to = move(y, c, z, x)
                        if to is not None:
                            moves.append((self.flat(y, c, z, x), self.flat(*to)))
        return lax.ppermute(value, AXES, moves)

    def flat(self, y, core, z, x):
        return (2 * (y % self.ny) + core) * self.no + z * self.nx + x % self.nx

    def other_core(self, value):
        return self.send(value, lambda y, c, z, x: (y, 1 - c, z, x))

    def shift(self, value, dy, dx):
        return self.send(value, lambda y, c, z, x: (y - dy, c, z, x - dx))


def after(value, *others):
    return lax.optimization_barrier((value, *others))[0]


def spread_windows(grid, groups, pick, owners):
    nx, nz = grid.nx, grid.nz
    low = grid.core == 0

    def from_owners(panels, pieces):
        rows = pieces[0].shape[0] // nx

        def cut(pair, x):
            return jnp.where(low, *(lax.dynamic_slice_in_dim(v, (x % nx) * rows, rows, 0) for v in pair))

        halves = []
        for dc in range(2):
            block = None
            for k in range(nx):
                piece = cut(pieces[::-1] if dc else pieces, grid.x + k)
                got = piece
                if (dc, k) != (0, 0):
                    got = grid.send(piece, lambda y, c, z, x: (y, c ^ dc, z, x + k) if z == 0 else None)
                source = (grid.x - k + nx) % nx
                fresh = [source == jnp.where(low, owners[0][p], owners[1][p]) for p in panels]
                fresh = jnp.repeat(jnp.stack(fresh), PB)[None, :]
                block = got if block is None else jnp.where(fresh, got, block)
            halves.append(block)
        return jnp.concatenate([jnp.where(low, *halves), jnp.where(low, *halves[::-1])], 0)

    def onward(part, step):
        got = grid.send(part, lambda y, c, z, x: (y, c, z + step, x) if z % (2 * step) == 0 else None)
        return jnp.where(grid.z % (2 * step) == step, got, part)

    def collect(part):
        return [part] + [
            grid.shift(part, dy, dx)
            for dy in range(grid.ny)
            for dx in range(nx)
            if (dy, dx) != (0, 0)
        ]

    steps = [nz >> i for i in range(1, nz.bit_length())]
    first = from_owners(groups[0], pick(groups[0], None))
    second = from_owners(groups[1], pick(groups[1], first))
    for step in steps:
        first = onward(first, step)
    windows = collect(first)
    second = after(second, first)
    for step in steps:
        second = onward(second, step)
    return windows, first, second, collect(second)


def local(activations, ffn_grads, lengths, sample_pos):
    n_dp, n_owner = lax.axis_size("dp"), lax.axis_size("owner")
    tokens = activations.shape[0]
    total = tokens * n_dp
    grid = Grid(n_dp, n_owner)
    doc_len = lengths[0]
    doc_start = jnp.cumsum(doc_len) - doc_len
    row_index = (doc_start[:, None] + jnp.remainder(sample_pos[0], doc_len[:, None])).reshape(-1)

    def weights(lens):
        scale = lens.astype(F32) / (SAMP_DOC * total)
        return jnp.broadcast_to(scale[..., None], (*lens.shape, SAMP_DOC)).reshape(-1, 1)

    weight = weights(doc_len)
    dp = lax.axis_index("dp")
    lens = jnp.zeros((n_dp, 1, doc_len.shape[0]), jnp.int32)
    for k in range(n_dp):
        there = lengths if k == 0 else lax.ppermute(lengths, "dp", [((i + k) % n_dp, i) for i in range(n_dp)])
        lens = jnp.where((jnp.arange(n_dp) == (dp + k) % n_dp)[:, None, None], there[None], lens)
    row_index, lens = lax.optimization_barrier((row_index, lens))
    every_weight = weights(lens.reshape(n_dp, -1))
    hot = (row_index[:, None] == jnp.arange(tokens, dtype=jnp.int32)[None, :]).astype(BF16)

    def pick(hot, values):
        return jnp.dot(hot, values, preferred_element_type=F32).astype(BF16)

    values = (activations, ffn_grads)
    owners = [[p * PB // v.shape[1] for p in range(NPAN)] for v in values]

    def pick_panels(panels, behind):
        rows = hot if behind is None else after(hot, behind)
        pieces = []
        for v in values:
            firsts = [p * PB % v.shape[1] for p in panels]
            pieces.append(pick(rows, jnp.concatenate([v[:, f : f + PB] for f in firsts], 1)))
        return pieces

    groups = ([0], list(range(1, NPAN)))
    window0, part0, part1, window1 = spread_windows(grid, groups, pick_panels, owners)

    nrows = SAMP_DOC * doc_len.shape[0]
    places = jnp.stack(
        [
            ((grid.y + dy) % grid.ny) * (2 * nrows) + ((grid.x + dx) % grid.nx) * (nrows // grid.nx)
            for dy in range(grid.ny)
            for dx in range(grid.nx)
        ]
        + [nrows]
    ).astype(jnp.int32)
    hot, weight = lax.optimization_barrier((hot, weight, part0))[:2]
    rows = jnp.concatenate([(weight * pick(hot, v).astype(F32)).astype(BF16) for v in values], axis=1)
    ahead = lax.optimization_barrier((*window0, part1, rows))[:-2]
    own, other = [], []
    for panel in range(NPAN):
        window, column = (ahead, 0) if panel == 0 else (window1, panel - 1)
        done = factor_panel(window, column, places, every_weight, own)
        own.append(done)
        other.append(grid.other_core(done))

    scaled, order = [], []
    for dy in range(grid.ny):
        here = rows if dy == 0 else grid.shift(after(rows, *window1, own[0]), dy, 0)
        scaled += [here, grid.other_core(here)]
        order += [(((grid.y + dy) % grid.ny) * 2 + core) * nrows for core in (grid.core, 1 - grid.core)]
    heights = [v.shape[1] for v in values]
    position = [grid.core, *(lax.axis_index("owner") * h for h in heights), *order]
    position = jnp.stack(position).astype(jnp.int32)
    outs = ()
    for panels in (list(range(NPAN - 1)), [NPAN - 1]):
        outs = factor_rows(scaled, heights, panels, position, own, other, outs)
    return tuple(outs)


def solution(mesh):
    return jax.shard_map(
        local,
        mesh=mesh,
        in_specs=(P("dp", "owner"), P("dp", "owner"), P("dp", None), P("dp", None, None)),
        out_specs=(P("owner", None), P("owner", None)),
        check_vma=False,
    )
```

```python
import functools

import jax
import jax.numpy as jnp
from jax import lax
from jax.experimental import pallas as pl
from jax.experimental.pallas import tpu as pltpu
from jax.sharding import PartitionSpec as P

PB = 512
NPAN = 3
SAMP_DOC = 16
DAMPING = 0.1
BLK = 128
TILE = 256
ROWS = 512
F32 = jnp.float32
BF16 = jnp.bfloat16
AXES = ("dp", "owner")


def split(x):
    hi = x.astype(BF16)
    return hi, (x - hi.astype(F32)).astype(BF16)


def mm(a, b, ca, cb):
    return lax.dot_general(a, b, (((ca,), (cb,)), ((), ())), preferred_element_type=F32)


def mm3(a, b, ca, cb):
    (ah, al), (bh, bl) = a, b
    return mm(jnp.concatenate([ah, ah, al], ca), jnp.concatenate([bh, bl, bh], cb), ca, cb)


def recip(d):
    r = pltpu.reciprocal(d, approx=True)
    return r * (2.0 - d * r)


def factor_block(a):
    lane = lax.broadcasted_iota(jnp.int32, (8, BLK), 1)
    sub = lax.broadcasted_iota(jnp.int32, (8, BLK), 0)
    groups = BLK // 8
    rows_of = [a[8 * g : 8 * g + 8] for g in range(groups)]
    upper, inverse = [], []

    def fill(x):
        return jnp.broadcast_to(x, (8, BLK))

    for g in range(groups):
        top, c0 = rows_of[g], 8 * g
        rr = [fill(top[i : i + 1, :]) for i in range(8)]
        e = {(i, j): fill(rr[i][:, c0 + j : c0 + j + 1]) for i in range(8) for j in range(i + 1)}
        below = range(g + 1, groups)
        unit, mult, solved = {}, {}, {}
        for k in range(0, 8, 2):
            p, q, r = e[k, k], e[k + 1, k], e[k + 1, k + 1]
            inv = recip(p * r - q * q)
            at0, at1 = lane == c0 + k, lane == c0 + k + 1
            s0 = jnp.where(at0, 1.0, jnp.where(at1, 0.0, rr[k]))
            s1 = jnp.where(at1, 1.0, jnp.where(at0, 0.0, rr[k + 1]))
            for i in range(k + 2, 8):
                x, y = e[i, k], e[i, k + 1]
                m0, m1 = (x * r - y * q) * inv, (y * p - x * q) * inv
                mult[i, k], mult[i, k + 1] = m0, m1
                for j in range(k + 2, i + 1):
                    e[i, j] = e[i, j] - (m0 * e[j, k] + m1 * e[j, k + 1])
                rr[i] = jnp.where(at0 | at1, 0.0, rr[i]) - (m0 * s0 + m1 * s1)
            later = (lane > c0 + k + 1) & (lane < c0 + 8)
            s0, s1 = jnp.where(later, 0.0, s0), jnp.where(later, 0.0, s1)
            unit[k], unit[k + 1] = (s0 * r - s1 * q) * inv, (s1 * p - s0 * q) * inv
        if g + 1 < groups:
            for k in range(6, -1, -2):
                for c in (k, k + 1):
                    t = unit[c]
                    for i in range(6, k, -2):
                        t = t - (mult[i, c] * solved[i] + mult[i + 1, c] * solved[i + 1])
                    solved[c] = t
        for h in below:
            col = [fill(rows_of[h][:, c0 + j : c0 + j + 1]) for j in range(8)]
            base = jnp.where((lane >= c0) & (lane < c0 + 8), 0.0, rows_of[h])
            pair = [col[j] * solved[j] + col[j + 1] * solved[j + 1] for j in range(0, 8, 2)]
            rows_of[h] = base - ((pair[0] + pair[1]) + (pair[2] + pair[3]))
        done = scale = None
        for k in range(8):
            if k % 2 == 0:
                d, row = e[k, k], rr[k]
            else:
                t = e[k, k - 1] / e[k - 1, k - 1]
                d = e[k, k] - t * e[k, k - 1]
                before = lane == c0 + k - 1
                row = jnp.where(before, 0.0, rr[k]) - t * jnp.where(before, 1.0, rr[k - 1])
            s = lax.rsqrt(d)
            row = row * s
            done = row if k == 0 else jnp.where(sub == k, row, done)
            scale = s if k == 0 else jnp.where(sub == k, s, scale)
        diag = c0 + sub
        upper.append(jnp.where(lane >= diag, done, 0.0))
        inverse.append(jnp.where(lane < diag, done, jnp.where(lane == diag, scale, 0.0)))
    return jnp.concatenate(upper, 0), jnp.concatenate(inverse, 0)


def pick_kernel(index_ref, a_ref, b_ref, a_out, b_out, hot):
    @pl.when(pl.program_id(0) == 0)
    def _():
        token = lax.broadcasted_iota(jnp.int32, hot.shape, 1)
        hot[...] = jnp.where(token == index_ref[...], 1.0, 0.0).astype(BF16)

    a_out[...] = mm(hot[...], a_ref[...], 1, 0).astype(BF16)
    b_out[...] = mm(hot[...], b_ref[...], 1, 0).astype(BF16)


def pick_columns(index, values, panels):
    rows, tokens, per = index.shape[0], values[0].shape[0], PB // TILE

    def column(width):
        firsts = [p * PB % width // TILE for p in panels]

        def at(i):
            first = firsts[0]
            for k in range(1, len(panels)):
                first = jnp.where(i // per == k, firsts[k], first)
            return (0, first + i % per)

        return at

    out = jax.ShapeDtypeStruct((rows, PB * len(panels)), BF16)
    return pl.pallas_call(
        pick_kernel,
        grid=(per * len(panels),),
        in_specs=[pl.BlockSpec((rows, 1), lambda i: (0, 0))]
        + [pl.BlockSpec((tokens, TILE), column(v.shape[1])) for v in values],
        out_specs=[pl.BlockSpec((rows, TILE), lambda i: (0, i))] * 2,
        out_shape=[out, out],
        scratch_shapes=[pltpu.VMEM((rows, tokens), BF16)],
        compiler_params=pltpu.CompilerParams(vmem_limit_bytes=16 << 20),
        name=f"pick_columns_{panels[0]}",
    )(index, *(pltpu.with_memory_space_constraint(v, pltpu.HBM) for v in values))


def panel_kernel(panel, blocks, place_ref, *refs):
    w_refs, weight_ref = refs[:blocks], refs[blocks]
    prev = refs[blocks + 1 : blocks + 1 + panel]
    v_ref, l_ref, w, swt, a, y, lq, xs = refs[blocks + 1 + panel :]
    samples = w.shape[0]
    known_rows = slice(0, samples)
    rows = samples // blocks
    half, apart = rows // 2, place_ref[blocks]
    for i in range(blocks):
        for core in range(2):
            at = pl.ds(pl.multiple_of(place_ref[i] + core * apart, half), half)
            w[at, :] = w_refs[i][core * half : (core + 1) * half, :]

    for i in range(samples // TILE):
        at = slice(i * TILE, (i + 1) * TILE)
        swt[:, at] = (weight_ref[at, :] * w[at, :].astype(F32)).astype(BF16).T

    gram = mm(swt[...], w[...], 1, 0)
    row = lax.broadcasted_iota(jnp.int32, (PB, PB), 0)
    column = lax.broadcasted_iota(jnp.int32, (PB, PB), 1)
    a[...] = 0.5 * (gram + gram.T) + jnp.where(row == column, DAMPING, 0.0)
    for q in range(panel):
        lpq = mm(swt[...], prev[q][0, known_rows], 1, 0) + mm(swt[...], prev[q][1, known_rows], 1, 0)
        lq[q, 0], lq[q, 1] = split(lpq)
    for j in range(PB // BLK):
        at, below = slice(j * BLK, (j + 1) * BLK), slice(j * BLK, PB)
        for q in range(panel):
            a[below, at] -= mm3((lq[q, 0, below], lq[q, 1, below]), (lq[q, 0, at], lq[q, 1, at]), 1, 1)

    l_ref[...] = jnp.zeros((PB, PB), F32)
    v_ref[...] = jnp.zeros(v_ref.shape, BF16)
    xs[...] = jnp.zeros(xs.shape, BF16)
    y[...] = jnp.zeros(y.shape, F32)

    def finish(at):
        found = y[...] - mm3((v_ref[0, known_rows], v_ref[1, known_rows]), split(l_ref[at, :]), 1, 1)
        v_ref[0, known_rows, at], v_ref[1, known_rows, at] = split(mm3(split(found), (xs[0], xs[1]), 1, 1))

    @pl.loop(0, PB // BLK)
    def _(b):
        at = pl.ds(pl.multiple_of(b * BLK, BLK), BLK)
        finish(pl.ds(pl.multiple_of(jnp.maximum(b - 1, 0) * BLK, BLK), BLK))
        own = w[:, at].astype(F32)
        for q in range(panel):
            own -= mm3((prev[q][0, known_rows], prev[q][1, known_rows]), (lq[q, 0, at, :], lq[q, 1, at, :]), 1, 1)
        y[...] = own
        upper, inverse = factor_block(a[at, at])
        x = split(inverse)
        xs[0], xs[1] = x
        l_ref[at, at] = upper.T
        for known in range(PB // BLK - 1):

            @pl.when(b == known)
            def _():
                done, below = slice(known * BLK, (known + 1) * BLK), slice((known + 1) * BLK, PB)
                lcol = mm3(split(a[below, done]), x, 1, 1)
                l_ref[below, done] = lcol
                lh, ll = split(lcol)
                for j in range(PB // BLK - known - 1):
                    c, r = slice(j * BLK, (j + 1) * BLK), slice((known + 1 + j) * BLK, PB)
                    to = slice((known + 1 + j) * BLK, (known + 2 + j) * BLK)
                    a[r, to] -= mm3((lh[j * BLK :], ll[j * BLK :]), (lh[c], ll[c]), 1, 1)

    finish(slice(PB - BLK, PB))
    v_ref[0, samples:, :], v_ref[1, samples:, :] = split(l_ref[...])


def factor_panel(window, column, places, weight, done):
    panel, samples = len(done), weight.shape[0]
    vshape = jax.ShapeDtypeStruct((2, samples + PB, PB), BF16)

    def whole(x):
        return pl.BlockSpec(x.shape, lambda i, place: (0,) * len(x.shape))

    return pl.pallas_call(
        functools.partial(panel_kernel, panel, len(window)),
        grid_spec=pltpu.PrefetchScalarGridSpec(
            num_scalar_prefetch=1,
            grid=(1,),
            in_specs=[pl.BlockSpec((b.shape[0], PB), lambda i, place: (0, column)) for b in window]
            + [whole(x) for x in (weight, *done)],
            out_specs=whole(vshape),
            scratch_shapes=[
                pltpu.VMEM((PB, PB), F32),
                pltpu.VMEM((samples, PB), BF16),
                pltpu.VMEM((PB, samples), BF16),
                pltpu.VMEM((PB, PB), F32),
                pltpu.VMEM((samples, BLK), F32),
                pltpu.VMEM((max(panel, 1), 2, PB, PB), BF16),
                pltpu.VMEM((2, BLK, BLK), BF16),
            ],
        ),
        out_shape=vshape,
        compiler_params=pltpu.CompilerParams(vmem_limit_bytes=(12 << 20) + (20 << 10) * samples),
        cost_estimate=pl.CostEstimate(flops=int(3e10), transcendentals=0, bytes_accessed=int(1e7)),
        name=f"factor_panel_{panel}",
    )(places, *window, weight, *done)


def rows_kernel(blocks, panels, tiles, pos_ref, *refs):
    n = len(panels)
    s_refs, own, other = refs[:blocks], refs[blocks : blocks + n], refs[blocks + n : blocks + 2 * n]
    out_refs, (st, buf, sem) = refs[-5:-3], refs[-3:]
    step = pl.program_id(0)
    rows = s_refs[0].shape[1]
    samples = rows * blocks

    def copies(m, group):
        return [pltpu.make_async_copy(group[p], buf.at[m, p], sem.at[m, p]) for p in range(n)]

    @pl.when(step == 0)
    def _():
        for core in range(2):

            @pl.when(pos_ref[0] == core)
            def _():
                for m in range(2):
                    for copy in copies(m, own if m == core else other):
                        copy.start()

    for j in range(blocks):
        st[:, pl.ds(pl.multiple_of(pos_ref[3 + j], rows), rows)] = s_refs[j][...]

    for m in range(2):

        @pl.when(step == (0 if m == 0 else tiles[0]))
        def _():
            for copy in copies(m, own):
                copy.wait()

        @pl.when((step < tiles[0]) if m == 0 else (step >= tiles[0]))
        def _():
            out_ref = out_refs[m]
            first = pos_ref[1 + m] + (step if m == 0 else step - tiles[0]) * ROWS
            for i, p in enumerate(panels):
                cols = slice(i * PB, (i + 1) * PB)

                @pl.when(first >= (p + 1) * PB)
                def _():
                    s = st[...]
                    total = mm(s, buf[m, i, 0, :samples], 1, 0) + mm(s, buf[m, i, 1, :samples], 1, 0)
                    out_ref[:, cols] = total

                @pl.when((first >= p * PB) & (first < (p + 1) * PB))
                def _():
                    at = pl.multiple_of(samples + jnp.clip(first - p * PB, 0, PB - ROWS), ROWS)
                    at = pl.ds(at, ROWS)
                    out_ref[:, cols] = buf[m, i, 0, at, :].astype(F32) + buf[m, i, 1, at, :].astype(F32)

                @pl.when(first < p * PB)
                def _():
                    out_ref[:, cols] = jnp.zeros((ROWS, PB), F32)


def factor_rows(scaled, heights, panels, position, own, other, into):
    n, samples = len(panels), sum(s.shape[1] for s in scaled)
    parts = [group[p] for group in (own, other) for p in panels]
    anywhere = pl.BlockSpec(memory_space=pl.ANY)
    tiles = [h // ROWS for h in heights]
    column = panels[0] // n

    def out_tile(m):
        if m == 0:
            return lambda i, pos: (jnp.minimum(i, tiles[0] - 1), column)
        return lambda i, pos: (jnp.maximum(i - tiles[0], 0), column)

    out_shape = [jax.ShapeDtypeStruct((h, NPAN * PB), F32) for h in heights]
    first_into = 1 + len(scaled) + len(parts)
    return pl.pallas_call(
        functools.partial(rows_kernel, len(scaled), panels, tiles),
        grid_spec=pltpu.PrefetchScalarGridSpec(
            num_scalar_prefetch=1,
            grid=(sum(tiles),),
            in_specs=[pl.BlockSpec((ROWS, s.shape[1]), lambda i, pos: (i, 0)) for s in scaled]
            + [anywhere] * (len(parts) + len(into)),
            out_specs=[pl.BlockSpec((ROWS, n * PB), out_tile(m)) for m in range(2)],
            scratch_shapes=[
                pltpu.VMEM((ROWS, samples), BF16),
                pltpu.VMEM((2, n, *own[0].shape), BF16),
                pltpu.SemaphoreType.DMA((2, n)),
            ],
        ),
        out_shape=out_shape,
        input_output_aliases={first_into + m: m for m in range(len(into))},
        compiler_params=pltpu.CompilerParams(vmem_limit_bytes=(20 << 20) + (16 << 10) * own[0].shape[1]),
        cost_estimate=pl.CostEstimate(
            flops=40 * n * samples * PB * sum(heights), transcendentals=0, bytes_accessed=4 * n * PB * sum(heights)
        ),
        name=f"factor_rows_{panels[0]}",
    )(position, *scaled, *parts, *into)


class Grid:
    def __init__(self, n_dp, n_owner):
        self.ny, self.no = n_dp // 2, n_owner
        self.nz = 4 if n_owner % 4 == 0 else 1
        self.nx = n_owner // self.nz
        dp, owner = lax.axis_index("dp"), lax.axis_index("owner")
        self.y, self.core = dp // 2, dp % 2
        self.z, self.x = owner // self.nx, owner % self.nx

    def send(self, value, move):
        moves = []
        for y in range(self.ny):
            for c in range(2):
                for z in range(self.nz):
                    for x in range(self.nx):
                        to = move(y, c, z, x)
                        if to is not None:
                            moves.append((self.flat(y, c, z, x), self.flat(*to)))
        return lax.ppermute(value, AXES, moves)

    def flat(self, y, core, z, x):
        return (2 * (y % self.ny) + core) * self.no + z * self.nx + x % self.nx

    def other_core(self, value):
        return self.send(value, lambda y, c, z, x: (y, 1 - c, z, x))

    def shift(self, value, dy, dx, dc=0):
        return self.send(value, lambda y, c, z, x: (y - dy, c ^ dc, z, x - dx))


def after(value, *others):
    return lax.optimization_barrier((value, *others))[0]


def spread_windows(grid, groups, pick, owners, lens, beside):
    nx, nz = grid.nx, grid.nz
    low = grid.core == 0

    def from_owners(panels, pieces):
        rows = pieces[0].shape[0] // nx

        def cut(pair, x):
            return jnp.where(low, *(lax.dynamic_slice_in_dim(v, (x % nx) * rows, rows, 0) for v in pair))

        halves = []
        for dc in range(2):
            block = None
            for k in range(nx):
                piece = cut(pieces[::-1] if dc else pieces, grid.x + k)
                got = piece
                if (dc, k) != (0, 0):
                    got = grid.send(piece, lambda y, c, z, x: (y, c ^ dc, z, x + k) if z == 0 else None)
                source = (grid.x - k + nx) % nx
                fresh = [source == jnp.where(low, owners[0][p], owners[1][p]) for p in panels]
                fresh = jnp.repeat(jnp.stack(fresh), PB)[None, :]
                block = got if block is None else jnp.where(fresh, got, block)
            halves.append(block)
        return jnp.concatenate([jnp.where(low, *halves), jnp.where(low, *halves[::-1])], 0)

    def onward(part, step):
        got = grid.send(part, lambda y, c, z, x: (y, c, z + step, x) if z % (2 * step) == 0 else None)
        return jnp.where(grid.z % (2 * step) == step, got, part)

    def collect(part):
        return [part] + [
            grid.shift(part, dy, dx)
            for dy in range(grid.ny)
            for dx in range(nx)
            if (dy, dx) != (0, 0)
        ]

    steps = [nz >> i for i in range(1, nz.bit_length())]
    first = from_owners(groups[0], pick(groups[0], None))
    second = from_owners(groups[1], pick(groups[1], first))
    for i, step in enumerate(steps):
        first = onward(first, step)
        if i == 0:
            first, lens = lax.optimization_barrier((first, lens))
    windows = collect(first)
    shared = beside(first)
    second = after(second, first)
    for step in steps:
        second = onward(second, step)
    return windows, second, collect(second), lens, shared


def local(activations, ffn_grads, lengths, sample_pos):
    n_dp, n_owner = lax.axis_size("dp"), lax.axis_size("owner")
    tokens = activations.shape[0]
    total = tokens * n_dp
    grid = Grid(n_dp, n_owner)
    doc_len = lengths[0]
    doc_start = jnp.cumsum(doc_len) - doc_len
    row_index = (doc_start[:, None] + jnp.remainder(sample_pos[0], doc_len[:, None])).reshape(-1)

    def weights(lens):
        scale = lens.astype(F32) / (SAMP_DOC * total)
        return jnp.broadcast_to(scale[..., None], (*lens.shape, SAMP_DOC)).reshape(-1, 1)

    weight = weights(doc_len)
    dp = lax.axis_index("dp")
    lens = jnp.zeros((n_dp, 1, doc_len.shape[0]), jnp.int32)
    for k in range(n_dp):
        there = lengths if k == 0 else lax.ppermute(lengths, "dp", [((i + k) % n_dp, i) for i in range(n_dp)])
        lens = jnp.where((jnp.arange(n_dp) == (dp + k) % n_dp)[:, None, None], there[None], lens)
    hot = (row_index[:, None] == jnp.arange(tokens, dtype=jnp.int32)[None, :]).astype(BF16)

    def pick(hot, values):
        return jnp.dot(hot, values, preferred_element_type=F32).astype(BF16)

    values = (activations, ffn_grads)
    owners = [[p * PB // v.shape[1] for p in range(NPAN)] for v in values]

    index = row_index[:, None].astype(jnp.int32)

    def pick_panels(panels, behind):
        return pick_columns(index if behind is None else after(index, behind), values, panels)

    def sample_rows(behind):
        late_hot, late_weight = lax.optimization_barrier((hot, weight, behind))[:2]
        rows = [(late_weight * pick(late_hot, v).astype(F32)).astype(BF16).T for v in values]
        return jnp.concatenate(rows, axis=0)

    groups = ([0], list(range(1, NPAN)))
    window0, part1, window1, lens, rows = spread_windows(
        grid, groups, pick_panels, owners, lens, sample_rows
    )
    every_weight = weights(lens.reshape(n_dp, -1))

    nrows = SAMP_DOC * doc_len.shape[0]
    places = jnp.stack(
        [
            ((grid.y + dy) % grid.ny) * (2 * nrows) + ((grid.x + dx) % grid.nx) * (nrows // grid.nx)
            for dy in range(grid.ny)
            for dx in range(grid.nx)
        ]
        + [nrows]
    ).astype(jnp.int32)
    ahead = lax.optimization_barrier((*window0, part1, rows))[: len(window0)]
    own, other, order = [], [], []
    for panel in range(NPAN):
        if panel == 1:
            late = after(rows, *window1, own[0])
            straight = [rows] + [grid.shift(late, dy, 0) for dy in range(1, grid.ny)]
            crossed = [grid.other_core(rows)]
        if panel == NPAN - 1:
            near = [*straight[1:], *crossed, *other[: panel - 1]]
            window1 = lax.optimization_barrier((*window1, *near))[: len(window1)]
            crossed += [grid.other_core(s) for s in straight[1:]]
        window, column = (ahead, 0) if panel == 0 else (window1, panel - 1)
        done = factor_panel(window, column, places, every_weight, own)
        own.append(done)
        other.append(grid.other_core(done))
    scaled = []
    for dy in range(grid.ny):
        scaled += [straight[dy], crossed[dy]]
        order += [(((grid.y + dy) % grid.ny) * 2 + core) * nrows for core in (grid.core, 1 - grid.core)]
    heights = [v.shape[1] for v in values]
    position = [grid.core, *(lax.axis_index("owner") * h for h in heights), *order]
    position = jnp.stack(position).astype(jnp.int32)
    outs = ()
    for panels in (list(range(NPAN - 1)), [NPAN - 1]):
        outs = factor_rows(scaled, heights, panels, position, own, other, outs)
    return tuple(outs)


def solution(mesh):
    return jax.shard_map(
        local,
        mesh=mesh,
        in_specs=(P("dp", "owner"), P("dp", "owner"), P("dp", None), P("dp", None, None)),
        out_specs=(P("owner", None), P("owner", None)),
        check_vma=False,
    )
```

```python
import functools

import jax
import jax.numpy as jnp
from jax import lax
from jax.experimental import pallas as pl
from jax.experimental.pallas import tpu as pltpu
from jax.sharding import PartitionSpec as P

PB = 512
NPAN = 3
SAMP_DOC = 16
DAMPING = 0.1
BLK = 128
TILE = 256
ROWS = 512
F32 = jnp.float32
BF16 = jnp.bfloat16
AXES = ("dp", "owner")


def split(x):
    hi = x.astype(BF16)
    return hi, (x - hi.astype(F32)).astype(BF16)


def mm(a, b, ca, cb):
    return lax.dot_general(a, b, (((ca,), (cb,)), ((), ())), preferred_element_type=F32)


def mm3(a, b, ca, cb):
    (ah, al), (bh, bl) = a, b
    return mm(jnp.concatenate([ah, ah, al], ca), jnp.concatenate([bh, bl, bh], cb), ca, cb)


def recip(d):
    r = pltpu.reciprocal(d, approx=True)
    return r * (2.0 - d * r)


def factor_block(a):
    lane = lax.broadcasted_iota(jnp.int32, (8, BLK), 1)
    sub = lax.broadcasted_iota(jnp.int32, (8, BLK), 0)
    groups = BLK // 8
    rows_of = [a[8 * g : 8 * g + 8] for g in range(groups)]
    upper, inverse = [], []

    def fill(x):
        return jnp.broadcast_to(x, (8, BLK))

    for g in range(groups):
        top, c0 = rows_of[g], 8 * g
        rr = [fill(top[i : i + 1, :]) for i in range(8)]
        e = {(i, j): fill(rr[i][:, c0 + j : c0 + j + 1]) for i in range(8) for j in range(i + 1)}
        below = range(g + 1, groups)
        unit, mult, solved = {}, {}, {}
        for k in range(0, 8, 2):
            p, q, r = e[k, k], e[k + 1, k], e[k + 1, k + 1]
            inv = recip(p * r - q * q)
            at0, at1 = lane == c0 + k, lane == c0 + k + 1
            s0 = jnp.where(at0, 1.0, jnp.where(at1, 0.0, rr[k]))
            s1 = jnp.where(at1, 1.0, jnp.where(at0, 0.0, rr[k + 1]))
            for i in range(k + 2, 8):
                x, y = e[i, k], e[i, k + 1]
                m0, m1 = (x * r - y * q) * inv, (y * p - x * q) * inv
                mult[i, k], mult[i, k + 1] = m0, m1
                for j in range(k + 2, i + 1):
                    e[i, j] = e[i, j] - (m0 * e[j, k] + m1 * e[j, k + 1])
                rr[i] = jnp.where(at0 | at1, 0.0, rr[i]) - (m0 * s0 + m1 * s1)
            later = (lane > c0 + k + 1) & (lane < c0 + 8)
            s0, s1 = jnp.where(later, 0.0, s0), jnp.where(later, 0.0, s1)
            unit[k], unit[k + 1] = (s0 * r - s1 * q) * inv, (s1 * p - s0 * q) * inv
        if g + 1 < groups:
            for k in range(6, -1, -2):
                for c in (k, k + 1):
                    t = unit[c]
                    for i in range(6, k, -2):
                        t = t - (mult[i, c] * solved[i] + mult[i + 1, c] * solved[i + 1])
                    solved[c] = t
        for h in below:
            col = [fill(rows_of[h][:, c0 + j : c0 + j + 1]) for j in range(8)]
            base = jnp.where((lane >= c0) & (lane < c0 + 8), 0.0, rows_of[h])
            pair = [col[j] * solved[j] + col[j + 1] * solved[j + 1] for j in range(0, 8, 2)]
            rows_of[h] = base - ((pair[0] + pair[1]) + (pair[2] + pair[3]))
        done = scale = None
        for k in range(8):
            if k % 2 == 0:
                d, row = e[k, k], rr[k]
            else:
                t = e[k, k - 1] / e[k - 1, k - 1]
                d = e[k, k] - t * e[k, k - 1]
                before = lane == c0 + k - 1
                row = jnp.where(before, 0.0, rr[k]) - t * jnp.where(before, 1.0, rr[k - 1])
            s = lax.rsqrt(d)
            row = row * s
            done = row if k == 0 else jnp.where(sub == k, row, done)
            scale = s if k == 0 else jnp.where(sub == k, s, scale)
        diag = c0 + sub
        upper.append(jnp.where(lane >= diag, done, 0.0))
        inverse.append(jnp.where(lane < diag, done, jnp.where(lane == diag, scale, 0.0)))
    return jnp.concatenate(upper, 0), jnp.concatenate(inverse, 0)


def pick_kernel(pos_ref, len_ref, a_ref, b_ref, a_out, b_out, index_out, hot):
    @pl.when(pl.program_id(0) == 0)
    def _():
        shape = (pos_ref.shape[0], len_ref.shape[1])
        doc = lax.broadcasted_iota(jnp.int32, shape, 0) // SAMP_DOC
        which = lax.broadcasted_iota(jnp.int32, shape, 1)
        lens = jnp.broadcast_to(len_ref[...].astype(F32), shape)
        length = jnp.sum(jnp.where(which == doc, lens, 0.0), axis=1, keepdims=True)
        start = jnp.sum(jnp.where(which < doc, lens, 0.0), axis=1, keepdims=True)
        pos = pos_ref[...].astype(F32)
        left = pos - jnp.floor(pos / length) * length
        left = jnp.where(left < 0.0, left + length, left)
        left = jnp.where(left >= length, left - length, left)
        index = (start + left).astype(jnp.int32)
        index_out[...] = index
        token = lax.broadcasted_iota(jnp.int32, hot.shape, 1)
        hot[...] = jnp.where(token == index, 1.0, 0.0).astype(BF16)

    a_out[...] = mm(hot[...], a_ref[...], 1, 0).astype(BF16)
    b_out[...] = mm(hot[...], b_ref[...], 1, 0).astype(BF16)


def pick_columns(pos, lengths, values, panels):
    rows, tokens, per = pos.shape[0], values[0].shape[0], PB // TILE

    def column(width):
        firsts = [p * PB % width // TILE for p in panels]

        def at(i):
            first = firsts[0]
            for k in range(1, len(panels)):
                first = jnp.where(i // per == k, firsts[k], first)
            return (0, first + i % per)

        return at

    out = jax.ShapeDtypeStruct((rows, PB * len(panels)), BF16)
    return pl.pallas_call(
        pick_kernel,
        grid=(per * len(panels),),
        in_specs=[pl.BlockSpec((rows, 1), lambda i: (0, 0)), pl.BlockSpec(lengths.shape, lambda i: (0, 0))]
        + [pl.BlockSpec((tokens, TILE), column(v.shape[1])) for v in values],
        out_specs=[pl.BlockSpec((rows, TILE), lambda i: (0, i))] * 2 + [pl.BlockSpec((rows, 1), lambda i: (0, 0))],
        out_shape=[out, out, jax.ShapeDtypeStruct((rows, 1), jnp.int32)],
        scratch_shapes=[pltpu.VMEM((rows, tokens), BF16)],
        compiler_params=pltpu.CompilerParams(vmem_limit_bytes=16 << 20),
        name=f"pick_columns_{panels[0]}",
    )(pos, lengths, *(pltpu.with_memory_space_constraint(v, pltpu.HBM) for v in values))


def panel_kernel(panel, blocks, place_ref, *refs):
    w_refs, weight_ref = refs[:blocks], refs[blocks]
    stored = refs[blocks + 1 : blocks + 1 + panel]
    v_ref, l_ref, w, swt, a, y, lq, xs, prev, sems = refs[blocks + 1 + panel :]
    samples = w.shape[0]
    known_rows = slice(0, samples)
    loads = [
        pltpu.make_async_copy(stored[q].at[part, known_rows], prev.at[q, part], sems.at[q, part])
        for q in range(panel)
        for part in range(2)
    ]
    for load in loads:
        load.start()
    rows = samples // blocks
    half, apart = rows // 2, place_ref[blocks]
    for i in range(blocks):
        for core in range(2):
            at = pl.ds(pl.multiple_of(place_ref[i] + core * apart, half), half)
            w[at, :] = w_refs[i][core * half : (core + 1) * half, :]

    for i in range(samples // TILE):
        at = slice(i * TILE, (i + 1) * TILE)
        swt[:, at] = (weight_ref[at, :] * w[at, :].astype(F32)).astype(BF16).T

    gram = mm(swt[...], w[...], 1, 0)
    row = lax.broadcasted_iota(jnp.int32, (PB, PB), 0)
    column = lax.broadcasted_iota(jnp.int32, (PB, PB), 1)
    a[...] = 0.5 * (gram + gram.T) + jnp.where(row == column, DAMPING, 0.0)
    for load in loads:
        load.wait()
    for q in range(panel):
        lpq = mm(swt[...], prev[q, 0], 1, 0) + mm(swt[...], prev[q, 1], 1, 0)
        lq[q, 0], lq[q, 1] = split(lpq)
    for j in range(PB // BLK):
        at, below = slice(j * BLK, (j + 1) * BLK), slice(j * BLK, PB)
        for q in range(panel):
            a[below, at] -= mm3((lq[q, 0, below], lq[q, 1, below]), (lq[q, 0, at], lq[q, 1, at]), 1, 1)

    l_ref[...] = jnp.zeros((PB, PB), F32)
    v_ref[...] = jnp.zeros(v_ref.shape, BF16)
    xs[...] = jnp.zeros(xs.shape, BF16)
    y[...] = jnp.zeros(y.shape, F32)

    def finish(at):
        found = y[...] - mm3((v_ref[0, known_rows], v_ref[1, known_rows]), split(l_ref[at, :]), 1, 1)
        v_ref[0, known_rows, at], v_ref[1, known_rows, at] = split(mm3(split(found), (xs[0], xs[1]), 1, 1))

    @pl.loop(0, PB // BLK)
    def _(b):
        at = pl.ds(pl.multiple_of(b * BLK, BLK), BLK)
        finish(pl.ds(pl.multiple_of(jnp.maximum(b - 1, 0) * BLK, BLK), BLK))
        own = w[:, at].astype(F32)
        for q in range(panel):
            own -= mm3((prev[q, 0], prev[q, 1]), (lq[q, 0, at, :], lq[q, 1, at, :]), 1, 1)
        y[...] = own
        upper, inverse = factor_block(a[at, at])
        x = split(inverse)
        xs[0], xs[1] = x
        l_ref[at, at] = upper.T
        for known in range(PB // BLK - 1):

            @pl.when(b == known)
            def _():
                done, below = slice(known * BLK, (known + 1) * BLK), slice((known + 1) * BLK, PB)
                lcol = mm3(split(a[below, done]), x, 1, 1)
                l_ref[below, done] = lcol
                lh, ll = split(lcol)
                for j in range(PB // BLK - known - 1):
                    c, r = slice(j * BLK, (j + 1) * BLK), slice((known + 1 + j) * BLK, PB)
                    to = slice((known + 1 + j) * BLK, (known + 2 + j) * BLK)
                    a[r, to] -= mm3((lh[j * BLK :], ll[j * BLK :]), (lh[c], ll[c]), 1, 1)

    finish(slice(PB - BLK, PB))
    v_ref[0, samples:, :], v_ref[1, samples:, :] = split(l_ref[...])


def factor_panel(window, column, places, weight, done):
    panel, samples = len(done), weight.shape[0]
    vshape = jax.ShapeDtypeStruct((2, samples + PB, PB), BF16)

    def whole(x):
        return pl.BlockSpec(x.shape, lambda i, place: (0,) * len(x.shape))

    return pl.pallas_call(
        functools.partial(panel_kernel, panel, len(window)),
        grid_spec=pltpu.PrefetchScalarGridSpec(
            num_scalar_prefetch=1,
            grid=(1,),
            in_specs=[pl.BlockSpec((b.shape[0], PB), lambda i, place: (0, column)) for b in window]
            + [whole(weight)]
            + [pl.BlockSpec(memory_space=pl.ANY)] * panel,
            out_specs=whole(vshape),
            scratch_shapes=[
                pltpu.VMEM((PB, PB), F32),
                pltpu.VMEM((samples, PB), BF16),
                pltpu.VMEM((PB, samples), BF16),
                pltpu.VMEM((PB, PB), F32),
                pltpu.VMEM((samples, BLK), F32),
                pltpu.VMEM((max(panel, 1), 2, PB, PB), BF16),
                pltpu.VMEM((2, BLK, BLK), BF16),
                pltpu.VMEM((max(panel, 1), 2, samples, PB), BF16),
                pltpu.SemaphoreType.DMA((max(panel, 1), 2)),
            ],
        ),
        out_shape=vshape,
        compiler_params=pltpu.CompilerParams(vmem_limit_bytes=(12 << 20) + (20 << 10) * samples),
        cost_estimate=pl.CostEstimate(flops=int(3e10), transcendentals=0, bytes_accessed=int(1e7)),
        name=f"factor_panel_{panel}",
    )(places, *window, weight, *done)


def rows_kernel(blocks, panels, tiles, pos_ref, *refs):
    n = len(panels)
    s_refs, own, other = refs[:blocks], refs[blocks : blocks + n], refs[blocks + n : blocks + 2 * n]
    out_refs, (buf, sem) = refs[-4:-2], refs[-2:]
    step = pl.program_id(0)
    rows = s_refs[0].shape[1]
    samples, per = rows * blocks, 2 * (blocks + 1)

    def copies(m, group):
        made = []
        for p in range(n):
            for part in range(2):
                for j in range(blocks):
                    at = pl.ds(pl.multiple_of(pos_ref[3 + j], rows), rows)
                    made.append((group[p].at[part, at], buf.at[m, p, part, j * rows : (j + 1) * rows]))
                made.append((group[p].at[part, samples:], buf.at[m, p, part, samples:]))
        return [pltpu.make_async_copy(s, d, sem.at[m, i]) for i, (s, d) in enumerate(made)]

    @pl.when(step == 0)
    def _():
        for core in range(2):

            @pl.when(pos_ref[0] == core)
            def _():
                for m in range(2):
                    for copy in copies(m, own if m == core else other):
                        copy.start()

    for m in range(2):

        @pl.when((step < tiles[0]) if m == 0 else (step >= tiles[0]))
        def _():
            out_ref = out_refs[m]
            first = pos_ref[1 + m] + (step if m == 0 else step - tiles[0]) * ROWS
            for i, p in enumerate(panels):
                cols = slice(i * PB, (i + 1) * PB)

                @pl.when(step == (0 if m == 0 else tiles[0]))
                def _():
                    for copy in copies(m, own)[i * per : (i + 1) * per]:
                        copy.wait()

                @pl.when(first >= (p + 1) * PB)
                def _():
                    s = jnp.concatenate([s_refs[j][...] for j in range(blocks)] * 2, 1)
                    v = jnp.concatenate([buf[m, i, part, :samples] for part in range(2)], 0)
                    out_ref[:, cols] = mm(s, v, 1, 0)

                @pl.when((first >= p * PB) & (first < (p + 1) * PB))
                def _():
                    at = pl.multiple_of(samples + jnp.clip(first - p * PB, 0, PB - ROWS), ROWS)
                    at = pl.ds(at, ROWS)
                    out_ref[:, cols] = buf[m, i, 0, at, :].astype(F32) + buf[m, i, 1, at, :].astype(F32)

                @pl.when(first < p * PB)
                def _():
                    out_ref[:, cols] = jnp.zeros((ROWS, PB), F32)


def factor_rows(scaled, heights, panels, position, own, other, into):
    n, samples = len(panels), sum(s.shape[1] for s in scaled)
    parts = [group[p] for group in (own, other) for p in panels]
    anywhere = pl.BlockSpec(memory_space=pl.ANY)
    tiles = [h // ROWS for h in heights]
    column = panels[0] // n

    def out_tile(m):
        if m == 0:
            return lambda i, pos: (jnp.minimum(i, tiles[0] - 1), column)
        return lambda i, pos: (jnp.maximum(i - tiles[0], 0), column)

    out_shape = [jax.ShapeDtypeStruct((h, NPAN * PB), F32) for h in heights]
    first_into = 1 + len(scaled) + len(parts)
    return pl.pallas_call(
        functools.partial(rows_kernel, len(scaled), panels, tiles),
        grid_spec=pltpu.PrefetchScalarGridSpec(
            num_scalar_prefetch=1,
            grid=(sum(tiles),),
            in_specs=[pl.BlockSpec((ROWS, s.shape[1]), lambda i, pos: (i, 0)) for s in scaled]
            + [anywhere] * (len(parts) + len(into)),
            out_specs=[pl.BlockSpec((ROWS, n * PB), out_tile(m)) for m in range(2)],
            scratch_shapes=[
                pltpu.VMEM((2, n, *own[0].shape), BF16),
                pltpu.SemaphoreType.DMA((2, 2 * n * (len(scaled) + 1))),
            ],
        ),
        out_shape=out_shape,
        input_output_aliases={first_into + m: m for m in range(len(into))},
        compiler_params=pltpu.CompilerParams(vmem_limit_bytes=(20 << 20) + (16 << 10) * own[0].shape[1]),
        cost_estimate=pl.CostEstimate(
            flops=40 * n * samples * PB * sum(heights), transcendentals=0, bytes_accessed=4 * n * PB * sum(heights)
        ),
        name=f"factor_rows_{panels[0]}",
    )(position, *scaled, *parts, *into)


class Grid:
    def __init__(self, n_dp, n_owner):
        self.ny, self.no = n_dp // 2, n_owner
        self.nz = 4 if n_owner % 4 == 0 else 1
        self.nx = n_owner // self.nz
        dp, owner = lax.axis_index("dp"), lax.axis_index("owner")
        self.y, self.core = dp // 2, dp % 2
        self.z, self.x = owner // self.nx, owner % self.nx

    def send(self, value, move):
        moves = []
        for y in range(self.ny):
            for c in range(2):
                for z in range(self.nz):
                    for x in range(self.nx):
                        to = move(y, c, z, x)
                        if to is not None:
                            moves.append((self.flat(y, c, z, x), self.flat(*to)))
        return lax.ppermute(value, AXES, moves)

    def flat(self, y, core, z, x):
        return (2 * (y % self.ny) + core) * self.no + z * self.nx + x % self.nx

    def other_core(self, value):
        return self.send(value, lambda y, c, z, x: (y, 1 - c, z, x))

    def shift(self, value, dy, dx, dc=0):
        return self.send(value, lambda y, c, z, x: (y - dy, c ^ dc, z, x - dx))


def after(value, *others):
    return lax.optimization_barrier((value, *others))[0]


def spread_windows(grid, groups, pick, owners, lens, beside):
    nx, nz = grid.nx, grid.nz
    low = grid.core == 0

    def from_owners(panels, pieces):
        rows = pieces[0].shape[0] // nx

        def cut(pair, x):
            return jnp.where(low, *(lax.dynamic_slice_in_dim(v, (x % nx) * rows, rows, 0) for v in pair))

        halves = []
        for dc in range(2):
            block = None
            for k in range(nx):
                piece = cut(pieces[::-1] if dc else pieces, grid.x + k)
                got = piece
                if (dc, k) != (0, 0):
                    got = grid.send(piece, lambda y, c, z, x: (y, c ^ dc, z, x + k) if z == 0 else None)
                source = (grid.x - k + nx) % nx
                fresh = [source == jnp.where(low, owners[0][p], owners[1][p]) for p in panels]
                fresh = jnp.repeat(jnp.stack(fresh), PB)[None, :]
                block = got if block is None else jnp.where(fresh, got, block)
            halves.append(block)
        return jnp.concatenate([jnp.where(low, *halves), jnp.where(low, *halves[::-1])], 0)

    def onward(part, step):
        got = grid.send(part, lambda y, c, z, x: (y, c, z + step, x) if z % (2 * step) == 0 else None)
        return jnp.where(grid.z % (2 * step) == step, got, part)

    def collect(part):
        return [part] + [
            grid.shift(part, dy, dx)
            for dy in range(grid.ny)
            for dx in range(nx)
            if (dy, dx) != (0, 0)
        ]

    steps = [nz >> i for i in range(1, nz.bit_length())]
    first = from_owners(groups[0], pick(groups[0], None))
    pieces = pick(groups[1], first)
    for i, step in enumerate(steps):
        first = onward(first, step)
        if i == 0:
            first, lens, *pieces = lax.optimization_barrier((first, lens, *pieces))
    second = from_owners(groups[1], pieces)
    windows = collect(first)
    shared = beside(first)
    second = after(second, first)
    for step in steps:
        second = onward(second, step)
    return windows, second, collect(second), lens, shared


def local(activations, ffn_grads, lengths, sample_pos):
    n_dp, n_owner = lax.axis_size("dp"), lax.axis_size("owner")
    tokens = activations.shape[0]
    total = tokens * n_dp
    grid = Grid(n_dp, n_owner)
    doc_len = lengths[0]

    def weights(lens):
        scale = lens.astype(F32) / (SAMP_DOC * total)
        return jnp.broadcast_to(scale[..., None], (*lens.shape, SAMP_DOC)).reshape(-1, 1)

    weight = weights(doc_len)
    dp = lax.axis_index("dp")
    lens = jnp.zeros((n_dp, 1, doc_len.shape[0]), jnp.int32)
    for k in range(n_dp):
        there = lengths if k == 0 else lax.ppermute(lengths, "dp", [((i + k) % n_dp, i) for i in range(n_dp)])
        lens = jnp.where((jnp.arange(n_dp) == (dp + k) % n_dp)[:, None, None], there[None], lens)

    def pick(hot, values):
        return jnp.dot(hot, values, preferred_element_type=F32).astype(BF16)

    values = (activations, ffn_grads)
    owners = [[p * PB // v.shape[1] for p in range(NPAN)] for v in values]

    pos = sample_pos.reshape(-1, 1)
    found = []

    def pick_panels(panels, behind):
        *pieces, index = pick_columns(pos if behind is None else after(pos, behind), lengths, values, panels)
        found.append(index)
        return pieces

    def sample_rows(behind):
        index, late_weight = lax.optimization_barrier((found[0], weight, behind))[:2]
        hot = (index == jnp.arange(tokens, dtype=jnp.int32)[None, :]).astype(BF16)
        rows = [(late_weight * pick(hot, v).astype(F32)).astype(BF16).T for v in values]
        return jnp.concatenate(rows, axis=0)

    groups = ([0], list(range(1, NPAN)))
    window0, part1, window1, lens, rows = spread_windows(
        grid, groups, pick_panels, owners, lens, sample_rows
    )
    every_weight = weights(lens.reshape(n_dp, -1))

    nrows = SAMP_DOC * doc_len.shape[0]
    places = jnp.stack(
        [
            ((grid.y + dy) % grid.ny) * (2 * nrows) + ((grid.x + dx) % grid.nx) * (nrows // grid.nx)
            for dy in range(grid.ny)
            for dx in range(grid.nx)
        ]
        + [nrows]
    ).astype(jnp.int32)
    ahead = lax.optimization_barrier((*window0, part1, rows))[: len(window0)]
    own, other, order = [], [], []
    for panel in range(NPAN):
        if panel == 1:
            late = after(rows, *window1, own[0])
            straight = [rows] + [grid.shift(late, dy, 0) for dy in range(1, grid.ny)]
            crossed = [grid.other_core(rows)]
        if panel == NPAN - 1:
            near = [*straight[1:], *crossed, *other[: panel - 1]]
            window1 = lax.optimization_barrier((*window1, *near))[: len(window1)]
            crossed += [grid.other_core(s) for s in straight[1:]]
        window, column = (ahead, 0) if panel == 0 else (window1, panel - 1)
        done = factor_panel(window, column, places, every_weight, own)
        own.append(done)
        other.append(grid.other_core(done))
    scaled = []
    for dy in range(grid.ny):
        scaled += [straight[dy], crossed[dy]]
        order += [(((grid.y + dy) % grid.ny) * 2 + core) * nrows for core in (grid.core, 1 - grid.core)]
    heights = [v.shape[1] for v in values]
    position = [grid.core, *(lax.axis_index("owner") * h for h in heights), *order]
    position = jnp.stack(position).astype(jnp.int32)
    outs = ()
    for panels in (list(range(NPAN - 1)), [NPAN - 1]):
        outs = factor_rows(scaled, heights, panels, position, own, other, outs)
    return tuple(outs)


def solution(mesh):
    return jax.shard_map(
        local,
        mesh=mesh,
        in_specs=(P("dp", "owner"), P("dp", "owner"), P("dp", None), P("dp", None, None)),
        out_specs=(P("owner", None), P("owner", None)),
        check_vma=False,
    )
```
